32 devices in a mesh: grp: 2 (over y), wide: 16 (over z, x, core).
Axes of the slice: x: 2, y: 2, z: 4, core: 2. Of those that a mesh axis runs over, the one named last changes fastest.
Arguments:
- activations: bfloat16 [2, 1024, 4096], P('grp', 'wide'), parts along dimension 0, may hold values from -6 to 6
- output_grads: bfloat16 [2, 1024, 4096], P('grp', None, 'wide'), parts along dimension 0, may hold values from -0.1875 to 0.1875
- token_ids: int32 [2, 1024], P('grp'), parts along dimension 0, may hold values from 0 to 128255, as said below
- row_signs: int32 [4096], replicated, may hold values from -1 to 1, as said below
- column_signs: int32 [4096], replicated, may hold values from -1 to 1, as said below
- kept_blocks: int32 [8192], P('wide'), may hold values from 0 to 131071, as said below
- queries: bfloat16 [256, 1048576], P(None, 'wide'), may hold values from -0.0078125 to 0.0078125
Outputs:
- sketches: bfloat16 [2, 1048576], P('grp', 'wide'), parts along dimension 0
- scores: float32 [256, 2], P('wide', 'grp'), parts along dimension 1
The draws below stay inside these ranges and needn't reach their ends.
There are 2 independent parts, one for each index of `grp`. The reference program is written for one: setup_inputs(seed, part) draws one part's arguments, and reference() takes and returns one part's arrays. A program takes and returns all parts, laid end to end along the dimension named above; an argument that names none is the same for every part. Nothing has to cross between parts.
Inputs may be any that keep to these rules, and one draw needn't show every extreme that they name: `token_ids`: id 0 marks padding. Each sequence ends with one run of one or more padding ids, and 512 or more of its ids are 1 or more. `row_signs`: every entry is +1 or -1. `column_signs`: every entry is +1 or -1. `kept_blocks`: A block number b names column b // 32 and rows (b % 32) * 128 up to (b % 32 + 1) * 128 - 1 of a sequence's projected matrix. For every d, entries d * 512 up to (d + 1) * 512 - 1 are distinct and name columns d * 256 up to (d + 1) * 256 - 1.
All inputs are finite; a program needn't handle non-finite values.
Results may differ from the reference program's by a relative error of at most 0.006.
Values may be sent and summed in bfloat16 or wider, within the bound.
A program may use at most 256 MiB of HBM per device.

```python
import jax
import jax.numpy as jnp
from jax import lax

D = 4096
ROWBLK = 128
K_BLOCKS = 8192
VOCAB = 128256
SEQS = 1
LEN = 1024
NQ = 256
COLS_DEV = 256
NBLK = 32
KEPT_DEV = 512
SKETCH = 1048576
N_WIDE = 16


def draw_token_ids(key, part):
    length_key = jax.random.fold_in(key, 13)
    token_key = jax.random.fold_in(key, 17)
    lengths = jax.random.randint(length_key, (SEQS,), LEN // 2, LEN)
    drawn = jax.random.randint(token_key, (SEQS, LEN), 1, VOCAB)
    positions = jnp.arange(LEN, dtype=jnp.int32)
    sequence_index = jnp.arange(SEQS, dtype=jnp.int32)
    topmost = (positions[None, :] == 0) & (sequence_index[:, None] == 0)
    drawn = jnp.where(topmost, VOCAB - 1, drawn)
    return jnp.where(positions[None, :] < lengths[:, None], drawn, 0).astype(jnp.int32)


def draw_row_signs(key, part):
    drawn = jax.random.randint(jax.random.fold_in(key, 11), (D,), 0, 2)
    return (2 * drawn - 1).astype(jnp.int32)


def draw_column_signs(key, part):
    drawn = jax.random.randint(jax.random.fold_in(key, 12), (D,), 0, 2)
    return (2 * drawn - 1).astype(jnp.int32)


def draw_kept_blocks(key, part):
    slab_keys = jax.random.split(jax.random.fold_in(key, 14), N_WIDE)
    per_slab = COLS_DEV * NBLK
    slab_index = jnp.arange(N_WIDE, dtype=jnp.int32)

    def one_slab(slab_key, slab_number):
        order = jax.random.permutation(slab_key, per_slab).astype(jnp.int32)
        target = jnp.where(slab_number == N_WIDE - 1, per_slab - 1, 0).astype(jnp.int32)
        places = jnp.arange(per_slab, dtype=jnp.int32)
        where_target = jnp.sum(jnp.where(order == target, places, 0)).astype(jnp.int32)
        first_value = order[0]
        swapped = jnp.where(places == 0, target, jnp.where(places == where_target, first_value, order))
        return swapped[:KEPT_DEV]
    chosen = jax.vmap(one_slab)(slab_keys, slab_index).astype(jnp.int32)
    offsets = slab_index[:, None] * per_slab
    return (chosen + offsets).reshape(K_BLOCKS).astype(jnp.int32)


def strengthened(entries, rng, source, target, shards_of, factor):
    def block_of(dim):
        return (jnp.arange(entries.shape[dim]) // (entries.shape[dim] // shards_of)).reshape((-1,) + (1,) * (entries.ndim - 1 - dim))

    first = jax.random.permutation(rng, shards_of)[block_of(target)]
    second = (block_of(target) + shards_of // 2) % shards_of
    return jnp.where((block_of(source) == first) | (block_of(source) == second), factor * entries, entries)


def shard_levels(rng, dims, cuts, least, top_value):
    def one(dim, blocks):
        heights = jax.random.uniform(jax.random.fold_in(jax.random.fold_in(rng, 6), dim), (blocks,), jnp.float32, least / len(cuts), top_value / len(cuts))
        return jnp.repeat(jnp.exp(heights), dims[dim] // blocks).reshape((-1,) + (1,) * (len(dims) - dim - 1))

    factor_of = one(*cuts[0])
    for cut in cuts[1:]:
        factor_of = factor_of * one(*cut)
    return factor_of


def normal_values(stream_key, dims, spread, reach, cuts=(), held_as=jnp.bfloat16):
    array = jax.random.normal(stream_key, dims, jnp.float32) * spread
    if len(cuts) > 0:
        array = shard_levels(stream_key, dims, cuts, -0.22, 0.18) * array
    return jnp.clip(array, min=-reach, max=reach).astype(held_as)


def gaussian_with(key, extent, scale, limit, pieces, heavy, kind=jnp.bfloat16):
    entries = scale * jax.random.normal(key, extent, jnp.float32)
    if pieces:
        entries = entries * shard_levels(key, extent, pieces, -0.22, 0.18)
    return jnp.clip(strengthened(entries, jax.random.fold_in(key, 3), *heavy), -limit, limit).astype(kind)


def setup_inputs(seed: int = 0, part: int = 0) -> dict:
    keys = jax.random.split(jax.random.key(seed), 8)
    part_splits = jax.random.split(jax.random.fold_in(keys[7], part), 8)
    activations = normal_values(part_splits[0], (SEQS, LEN, D), 1.0, 6.0, ((1, 16),))
    output_grads = normal_values(part_splits[1], (SEQS, LEN, D), LEN ** -0.5, 0.1875, ((2, 16),))
    token_ids = draw_token_ids(jax.random.fold_in(jax.random.fold_in(keys[7], part), 71), part)
    row_signs = draw_row_signs(jax.random.fold_in(keys[7], 71), part)
    column_signs = draw_column_signs(jax.random.fold_in(keys[7], 71), part)
    kept_blocks = draw_kept_blocks(jax.random.fold_in(keys[7], 71), part)
    queries = gaussian_with(keys[6], (NQ, SKETCH), SKETCH ** -0.5, 0.0078125, ((1, 16),), (1, 0, 16, 2.0))
    return dict(activations=activations, output_grads=output_grads, token_ids=token_ids, row_signs=row_signs, column_signs=column_signs, kept_blocks=kept_blocks, queries=queries)


def sign_table(bit_count):
    length = 2 ** bit_count
    indices = jnp.arange(length, dtype=jnp.int32)
    common = jnp.bitwise_and(indices[:, None], indices[None, :])
    parity = jnp.zeros((length, length), jnp.int32)
    for position in range(bit_count):
        parity = parity + jnp.bitwise_and(jnp.right_shift(common, position), 1)
    signs = 1 - 2 * jnp.bitwise_and(parity, 1)
    return (signs.astype(jnp.float32) * (length ** -0.5)).astype(jnp.bfloat16)


def hadamard_table(order_size):
    total_bits = order_size.bit_length() - 1
    low_bits = total_bits // 2
    high_table = sign_table(total_bits - low_bits)
    low_table = sign_table(low_bits)
    high_table, low_table = lax.optimization_barrier((high_table, low_table))
    return (high_table[:, None, :, None] * low_table[None, :, None, :]).reshape(order_size, order_size)


def reference(activations, output_grads, token_ids, row_signs, column_signs, kept_blocks, queries):
    hadamard = hadamard_table(D)
    hadamard_wide = hadamard.astype(jnp.float32)
    row_blocks = D // ROWBLK
    column_sign = column_signs.astype(jnp.bfloat16)
    row_sign = row_signs.astype(jnp.bfloat16)

    def one_sequence(sequence_inputs):
        activation_rows, gradient_rows, token_row = sequence_inputs
        weight = (token_row != 0).astype(jnp.bfloat16)
        signed_inputs = (activation_rows * column_sign[None, :]).astype(jnp.float32)
        turned = jnp.dot(signed_inputs, hadamard_wide,
                         preferred_element_type=jnp.float32).astype(jnp.bfloat16)
        weighted = (gradient_rows * weight[:, None]).astype(jnp.float32)
        half_turned = jnp.dot(weighted.T, turned.astype(jnp.float32),
                              preferred_element_type=jnp.float32).astype(jnp.bfloat16)
        signed = (half_turned * row_sign[:, None]).astype(jnp.float32)
        projected = jnp.dot(hadamard_wide, signed, preferred_element_type=jnp.float32)
        block_rows = projected.T.reshape(D * row_blocks, ROWBLK)
        picked = jnp.take(block_rows, kept_blocks.astype(jnp.int32), axis=0)
        return picked.reshape(K_BLOCKS * ROWBLK).astype(jnp.bfloat16)

    sketches = lax.map(one_sequence, (activations, output_grads, token_ids))
    scores = jnp.dot(queries.astype(jnp.float32), sketches.astype(jnp.float32).T,
                     preferred_element_type=jnp.float32)
    return sketches, scores
```

```python
import functools

import jax
import jax.numpy as jnp
from jax import lax
from jax.experimental import pallas as pl
from jax.experimental.pallas import tpu as pltpu
from jax.sharding import PartitionSpec as P

ROWBLK = 128


def sign_table(bit_count):
    length = 2**bit_count
    indices = jnp.arange(length, dtype=jnp.int32)
    common = jnp.bitwise_and(indices[:, None], indices[None, :])
    parity = jnp.zeros((length, length), jnp.int32)
    for position in range(bit_count):
        parity = parity + jnp.bitwise_and(jnp.right_shift(common, position), 1)
    signs = 1 - 2 * jnp.bitwise_and(parity, 1)
    return (signs.astype(jnp.float32) * length ** (-0.5)).astype(jnp.bfloat16)


def hadamard_table(order_size):
    total_bits = order_size.bit_length() - 1
    low_bits = total_bits // 2
    high_table = sign_table(total_bits - low_bits)
    low_table = sign_table(low_bits)
    high_table, low_table = lax.optimization_barrier((high_table, low_table))
    return (high_table[:, None, :, None] * low_table[None, :, None, :]).reshape(
        order_size, order_size
    )


def per_device_plain(activations, output_grads, token_ids, row_signs, column_signs, kept_blocks, queries):
    model_width = column_signs.shape[0]
    hadamard = hadamard_table(model_width)
    row_blocks = model_width // ROWBLK
    column_sign = column_signs.astype(jnp.bfloat16)
    row_sign = row_signs.astype(jnp.bfloat16)
    weight = (token_ids != 0).astype(jnp.bfloat16)
    columns_dev = output_grads.shape[2]
    device = lax.axis_index("wide")
    local_blocks = kept_blocks - device * (columns_dev * row_blocks)
    turned = jnp.einsum(
        "stj,jk->stk",
        activations * column_sign[None, None, :],
        hadamard,
        preferred_element_type=jnp.float32,
    ).astype(jnp.bfloat16)
    columns = lax.all_to_all(turned, "wide", split_axis=2, concat_axis=1, tiled=True)
    weighted = columns * weight[:, :, None]
    half_turned = jnp.einsum(
        "stc,sti->sci",
        weighted,
        lax.all_gather(output_grads, "wide", axis=2, tiled=True),
        preferred_element_type=jnp.float32,
    ).astype(jnp.bfloat16)
    signed = half_turned * row_sign[None, None, :]
    projected = jnp.einsum("scj,ji->sci", signed, hadamard, preferred_element_type=jnp.float32)
    items = projected.shape[0]
    block_rows = projected.reshape(items, projected.shape[1] * row_blocks, ROWBLK)
    picked = jnp.take(block_rows, local_blocks, axis=1)
    sketches = picked.reshape(items, picked.shape[1] * ROWBLK).astype(jnp.bfloat16)
    scores = lax.psum_scatter(
        jnp.einsum("qc,sc->qs", queries, sketches, preferred_element_type=jnp.float32),
        "wide",
        scatter_dimension=0,
        tiled=True,
    )
    return (sketches, scores)


def signs(size):
    common = jnp.bitwise_and(
        lax.broadcasted_iota(jnp.int32, (size, size), 0),
        lax.broadcasted_iota(jnp.int32, (size, size), 1),
    )
    shift = 1
    while shift < size:
        common = jnp.bitwise_xor(common, jnp.right_shift(common, shift))
        shift *= 2
    return (1 - 2 * jnp.bitwise_and(common, 1)).astype(jnp.float32).astype(jnp.bfloat16)


def butterflies(values):
    values = list(values)
    step = 1
    while step < len(values):
        for low in range(len(values)):
            if low & step == 0:
                first, second = values[low], values[low + step]
                values[low], values[low + step] = first + second, first - second
        step *= 2
    return values


def kernel(
    n, x_hbm, g_hbm, weight, column_sign, row_sign, kept, q_hbm,
    sk_ref, score_ref,
    xs, gs, kb, wide_f32, tall_f32, turned, left, spread, out_box, in_box, total, q_box, skf, part, part_in,
    x_sem, own_sem, q_sem, g_send, g_recv, r_send, r_recv, k_send, k_recv, p_send, p_recv, s_send, s_recv,
):
    me = lax.axis_index("wide")
    core = lax.rem(me, 2)
    chip = lax.div(me, 2)
    partner = me + 1 - 2 * core
    chips = n // 2
    tokens = x_hbm.shape[0]
    pair_tokens = 2 * tokens
    width = n * g_hbm.shape[1]
    cols = g_hbm.shape[1]
    kept_dev = kept.shape[1]
    row_blocks = width // ROWBLK
    per_high = cols // ROWBLK
    q_pieces = q_box.shape[0]
    q_cols = q_box.shape[2]
    scale = width**-0.5
    mine = pl.ds(pl.multiple_of(core * tokens, tokens), tokens)

    def remote(src, dst, send, recv, device):
        return pltpu.make_async_remote_copy(
            src_ref=src, dst_ref=dst, send_sem=send, recv_sem=recv,
            device_id={"wide": device}, device_id_type=pl.DeviceIdType.MESH,
        )

    def grad_copy(source, device):
        rows = pl.ds(pl.multiple_of(device * tokens, tokens), tokens)
        half = pl.ds(pl.multiple_of(lax.rem(device, 2) * tokens, tokens), tokens)
        return remote(g_hbm.at[rows, :], gs.at[source, half, :], g_send.at[device], g_recv.at[source], device)

    def relay_copy(source):
        return remote(gs.at[source, mine, :], gs.at[source, mine, :], r_send.at[source], r_recv.at[source], partner)

    def kept_copy(source, device):
        return remote(kept, kb.at[source], k_send.at[device], k_recv.at[source], device)

    def part_copy(slot, source_chip, device):
        return remote(out_box.at[slot], in_box.at[source_chip], p_send.at[slot], p_recv.at[source_chip], device)

    def score_copy(source, device):
        count = part_in.shape[1]
        rows = pl.ds(pl.multiple_of(device * count, count), count)
        return remote(part.at[rows, :], part_in.at[source], s_send.at[device], s_recv.at[source], device)

    x_local = pltpu.make_async_copy(x_hbm, xs.at[mine, :], own_sem.at[0])
    x_local.start()
    own_rows = pl.ds(pl.multiple_of(me * tokens, tokens), tokens)
    g_local = pltpu.make_async_copy(g_hbm.at[own_rows, :], gs.at[me, mine, :], own_sem.at[1])
    g_local.start()

    barrier = pltpu.get_barrier_semaphore()

    @pl.loop(1, n)
    def _(step):
        pl.semaphore_signal(
            barrier, inc=1, device_id={"wide": lax.rem(me + step, n)}, device_id_type=pl.DeviceIdType.MESH
        )

    pl.semaphore_wait(barrier, n - 1)

    x_pair = remote(x_hbm, xs.at[mine, :], x_sem.at[0], x_sem.at[1], partner)
    x_pair.start()

    @pl.loop(1, n)
    def _(step):
        grad_copy(me, lax.rem(me + step, n)).start()

    @pl.loop(1, chips)
    def _(step):
        kept_copy(me, lax.rem(me + 2 * step, n)).start()

    def query_copy(piece):
        begin = pl.multiple_of(piece * q_cols, q_cols)
        return pltpu.make_async_copy(q_hbm.at[:, pl.ds(begin, q_cols)], q_box.at[piece], q_sem.at[piece])

    @pl.loop(0, q_pieces)
    def _(piece):
        query_copy(piece).start()

    kb[me] = kept[...]
    table = signs(cols)
    x_local.wait()
    x_pair.wait()
    token_weight = weight[...]
    for block in range(n):
        lanes = slice(block * cols, (block + 1) * cols)
        signed = xs[:, lanes].astype(jnp.float32) * token_weight * column_sign[:, lanes].astype(jnp.float32)
        wide_f32[block] = jnp.dot(signed.astype(jnp.bfloat16), table, preferred_element_type=jnp.float32)

    @pl.loop(0, pair_tokens // 16)
    def _(tile):
        rows = pl.ds(pl.multiple_of(tile * 16, 16), 16)
        for lane in range(0, cols, 128):
            lanes = slice(lane, lane + 128)
            mixed = butterflies([wide_f32[block, rows, lanes] for block in range(n)])
            for block in range(n):
                turned[block, rows, lanes] = (mixed[block] * scale).astype(jnp.bfloat16)

    g_local.wait()
    relay_copy(me).start()

    @pl.loop(1, n)
    def _(step):
        source = lax.rem(me + n - step, n)
        grad_copy(source, me).wait_recv()
        relay_copy(source).start()

    for block in range(n):
        relay_copy(block).wait_recv()
        lanes = slice(block * cols, (block + 1) * cols)
        signed = (gs[block].astype(jnp.float32) * row_sign[:, lanes].astype(jnp.float32)).astype(jnp.bfloat16)
        tall_f32[block] = lax.dot_general(
            table, signed, (((1,), (1,)), ((), ())), preferred_element_type=jnp.float32
        )

    @pl.loop(0, cols // 16)
    def _(tile):
        rows = pl.ds(pl.multiple_of(tile * 16, 16), 16)
        for lane in range(0, pair_tokens, 128):
            lanes = slice(lane, lane + 128)
            mixed = butterflies([tall_f32[block, rows, lanes] for block in range(n)])
            for block in range(n):
                begin = block * pair_tokens + lane
                left[rows, begin : begin + 128] = (mixed[block] * scale).astype(jnp.bfloat16)

    def contribution(device):
        local = kb[device] - device * (cols * row_blocks)
        column = jnp.right_shift(local, row_blocks.bit_length() - 1)
        row = jnp.bitwise_and(local, row_blocks - 1)
        high = jnp.right_shift(row, per_high.bit_length() - 1)
        low = jnp.bitwise_and(row, per_high - 1)
        hit = lax.broadcasted_iota(jnp.int32, (cols, kept_dev), 0) == column
        chosen = jnp.dot(
            turned[device],
            jnp.where(hit, 1.0, 0.0).astype(jnp.bfloat16),
            preferred_element_type=jnp.float32,
        )
        for block in range(n):
            spread[block * pair_tokens : (block + 1) * pair_tokens, :] = jnp.where(high == block, chosen, 0.0).astype(
                jnp.bfloat16
            )
        full = jnp.dot(left[...], spread[...], preferred_element_type=jnp.float32)
        result = full[:ROWBLK]
        for block in range(1, per_high):
            result = jnp.where(low == block, full[block * ROWBLK : (block + 1) * ROWBLK], result)
        return result

    @pl.loop(1, chips)
    def _(step):
        target = lax.rem(me + 2 * step, n)
        kept_copy(target, me).wait_recv()
        out_box[step] = contribution(target).astype(jnp.bfloat16)
        part_copy(step, chip, target).start()

    total[...] = contribution(me)

    @pl.loop(1, chips)
    def _(step):
        source = lax.rem(chip + chips - step, chips)
        part_copy(step, source, me).wait_recv()
        total[...] += in_box[source].astype(jnp.float32)

    rounded = total[...].T.astype(jnp.bfloat16)
    sk_ref[...] = rounded
    skf[...] = rounded.astype(jnp.float32)
    part[...] = jnp.zeros_like(part)
    blocks_piece = q_cols // ROWBLK
    group = 4
    tall = 64

    @pl.loop(0, q_pieces)
    def _(piece):
        query_copy(piece).wait()
        for top in range(0, part.shape[0], tall):
            def body(index, acc):
                for extra in range(group):
                    block = index * group + extra
                    lanes = pl.ds(pl.multiple_of(block * ROWBLK, ROWBLK), ROWBLK)
                    line = skf[pl.ds(piece * blocks_piece + block, 1), :]
                    acc = acc + q_box[piece, top : top + tall, lanes].astype(jnp.float32) * line
                return acc

            part[top : top + tall, :] = lax.fori_loop(0, blocks_piece // group, body, part[top : top + tall, :])

    @pl.loop(1, n)
    def _(step):
        score_copy(me, lax.rem(me + step, n)).start()

    count = part_in.shape[1]
    part_in[me] = part[pl.ds(pl.multiple_of(me * count, count), count), :]

    @pl.loop(1, n)
    def _(step):
        score_copy(lax.rem(me + step, n), me).wait_recv()

    summed = part_in[0]
    for block in range(1, n):
        summed = summed + part_in[block]
    score_ref[...] = jnp.sum(summed, axis=1, keepdims=True)


    @pl.loop(1, n)
    def _(step):
        device = lax.rem(me + step, n)
        grad_copy(me, device).wait_send()
        score_copy(me, device).wait_send()

    @pl.loop(0, n)
    def _(step):
        relay_copy(step).wait_send()

    @pl.loop(1, chips)
    def _(step):
        kept_copy(me, lax.rem(me + 2 * step, n)).wait_send()
        part_copy(step, chip, lax.rem(me + 2 * step, n)).wait_send()


def per_device(n, activations, output_grads, token_ids, row_signs, column_signs, kept_blocks, queries):
    items, tokens, width = activations.shape
    cols = output_grads.shape[2]
    kept_dev = kept_blocks.shape[0]
    nq = queries.shape[0]
    q_pieces = 8
    fits = (
        items == 1
        and n % 2 == 0
        and n & (n - 1) == 0
        and cols & (cols - 1) == 0
        and cols % ROWBLK == 0
        and tokens % 16 == 0
        and (2 * tokens) % 128 == 0
        and kept_dev % 128 == 0
        and nq % (8 * n) == 0
        and nq % 64 == 0
        and kept_dev % (4 * q_pieces) == 0
        and queries.size * 2 <= 2**25
    )
    if not fits:
        return per_device_plain(
            activations, output_grads, token_ids, row_signs, column_signs, kept_blocks, queries
        )
    chips = n // 2
    chip = lax.div(lax.axis_index("wide"), 2)
    ids = lax.dynamic_slice(token_ids[0], (chip * 2 * tokens,), (2 * tokens,))
    weight = (ids != 0).astype(jnp.float32)[:, None]
    bf16, f32 = jnp.bfloat16, jnp.float32
    dma = pltpu.SemaphoreType.DMA
    any_spec = pl.BlockSpec(memory_space=pl.ANY)
    vmem_spec = pl.BlockSpec(memory_space=pltpu.VMEM)
    sketches, scores = pl.pallas_call(
        functools.partial(kernel, n),
        out_shape=(
            jax.ShapeDtypeStruct((kept_dev, ROWBLK), bf16),
            jax.ShapeDtypeStruct((nq // n, 1), f32),
        ),
        in_specs=[any_spec, any_spec, vmem_spec, vmem_spec, vmem_spec, vmem_spec, any_spec],
        out_specs=(vmem_spec, vmem_spec),
        scratch_shapes=[
            pltpu.VMEM((2 * tokens, width), bf16),
            pltpu.VMEM((n, 2 * tokens, cols), bf16),
            pltpu.VMEM((n, 1, kept_dev), jnp.int32),
            pltpu.VMEM((n, 2 * tokens, cols), f32),
            pltpu.VMEM((n, cols, 2 * tokens), f32),
            pltpu.VMEM((n, 2 * tokens, cols), bf16),
            pltpu.VMEM((cols, n * 2 * tokens), bf16),
            pltpu.VMEM((n * 2 * tokens, kept_dev), bf16),
            pltpu.VMEM((chips, ROWBLK, kept_dev), bf16),
            pltpu.VMEM((chips, ROWBLK, kept_dev), bf16),
            pltpu.VMEM((ROWBLK, kept_dev), f32),
            pltpu.VMEM((q_pieces, nq, queries.shape[1] // q_pieces), bf16),
            pltpu.VMEM((kept_dev, ROWBLK), f32),
            pltpu.VMEM((nq, ROWBLK), f32),
            pltpu.VMEM((n, nq // n, ROWBLK), f32),
            dma((2,)), dma((2,)), dma((q_pieces,)),
            dma((n,)), dma((n,)), dma((n,)), dma((n,)), dma((n,)), dma((n,)),
            dma((chips,)), dma((chips,)), dma((n,)), dma((n,)),
        ],
        compiler_params=pltpu.CompilerParams(
            collective_id=0, has_side_effects=True, vmem_limit_bytes=60 * 2**20
        ),
    )(
        activations[0],
        output_grads[0],
        weight,
        column_signs.astype(bf16)[None, :],
        row_signs.astype(bf16)[None, :],
        kept_blocks[None, :],
        queries,
    )
    return sketches.reshape(1, kept_dev * ROWBLK), scores


def solution(mesh):
    placed = (
        P("grp", "wide", None),
        P("grp", None, "wide"),
        P("grp", None),
        P(),
        P(),
        P("wide"),
        P(None, "wide"),
    )
    return jax.shard_map(
        functools.partial(per_device, mesh.shape["wide"]),
        mesh=mesh,
        in_specs=placed,
        out_specs=(P("grp", "wide"), P("wide", "grp")),
        check_vma=False,
    )
```

```python
import functools

import jax
import jax.numpy as jnp
from jax import lax
from jax.experimental import pallas as pl
from jax.experimental.pallas import tpu as pltpu
from jax.sharding import PartitionSpec as P

ROWBLK = 128


def sign_table(bit_count):
    length = 2**bit_count
    indices = jnp.arange(length, dtype=jnp.int32)
    common = jnp.bitwise_and(indices[:, None], indices[None, :])
    parity = jnp.zeros((length, length), jnp.int32)
    for position in range(bit_count):
        parity = parity + jnp.bitwise_and(jnp.right_shift(common, position), 1)
    signs = 1 - 2 * jnp.bitwise_and(parity, 1)
    return (signs.astype(jnp.float32) * length ** (-0.5)).astype(jnp.bfloat16)


def hadamard_table(order_size):
    total_bits = order_size.bit_length() - 1
    low_bits = total_bits // 2
    high_table = sign_table(total_bits - low_bits)
    low_table = sign_table(low_bits)
    high_table, low_table = lax.optimization_barrier((high_table, low_table))
    return (high_table[:, None, :, None] * low_table[None, :, None, :]).reshape(
        order_size, order_size
    )


def per_device_plain(activations, output_grads, token_ids, row_signs, column_signs, kept_blocks, queries):
    model_width = column_signs.shape[0]
    hadamard = hadamard_table(model_width)
    row_blocks = model_width // ROWBLK
    column_sign = column_signs.astype(jnp.bfloat16)
    row_sign = row_signs.astype(jnp.bfloat16)
    weight = (token_ids != 0).astype(jnp.bfloat16)
    columns_dev = output_grads.shape[2]
    device = lax.axis_index("wide")
    local_blocks = kept_blocks - device * (columns_dev * row_blocks)
    turned = jnp.einsum(
        "stj,jk->stk",
        activations * column_sign[None, None, :],
        hadamard,
        preferred_element_type=jnp.float32,
    ).astype(jnp.bfloat16)
    columns = lax.all_to_all(turned, "wide", split_axis=2, concat_axis=1, tiled=True)
    weighted = columns * weight[:, :, None]
    half_turned = jnp.einsum(
        "stc,sti->sci",
        weighted,
        lax.all_gather(output_grads, "wide", axis=2, tiled=True),
        preferred_element_type=jnp.float32,
    ).astype(jnp.bfloat16)
    signed = half_turned * row_sign[None, None, :]
    projected = jnp.einsum("scj,ji->sci", signed, hadamard, preferred_element_type=jnp.float32)
    items = projected.shape[0]
    block_rows = projected.reshape(items, projected.shape[1] * row_blocks, ROWBLK)
    picked = jnp.take(block_rows, local_blocks, axis=1)
    sketches = picked.reshape(items, picked.shape[1] * ROWBLK).astype(jnp.bfloat16)
    scores = lax.psum_scatter(
        jnp.einsum("qc,sc->qs", queries, sketches, preferred_element_type=jnp.float32),
        "wide",
        scatter_dimension=0,
        tiled=True,
    )
    return (sketches, scores)


def signs(size):
    common = jnp.bitwise_and(
        lax.broadcasted_iota(jnp.int32, (size, size), 0),
        lax.broadcasted_iota(jnp.int32, (size, size), 1),
    )
    shift = 1
    while shift < size:
        common = jnp.bitwise_xor(common, jnp.right_shift(common, shift))
        shift *= 2
    return (1 - 2 * jnp.bitwise_and(common, 1)).astype(jnp.float32).astype(jnp.bfloat16)


def butterflies(values):
    values = list(values)
    step = 1
    while step < len(values):
        for low in range(len(values)):
            if low & step == 0:
                first, second = values[low], values[low + step]
                values[low], values[low + step] = first + second, first - second
        step *= 2
    return values


def kernel(
    n, x_hbm, g_hbm, ids, column_sign, row_sign, kept, q_hbm,
    sk_ref, score_ref,
    xs, gs, kb, wide_f32, tall_f32, turned, left, spread, out_a, in_a, out_b, in_b, total, q_box, skf, part, part_in,
    x_sem, own_sem, q_sem, g_send, g_recv, r_send, r_recv, k_send, k_recv, a_send, a_recv, b_send, b_recv, s_send, s_recv,
):
    me = lax.axis_index("wide")
    core = lax.rem(me, 2)
    chip = lax.div(me, 2)
    partner = me + 1 - 2 * core
    chips = n // 2
    tokens = x_hbm.shape[0]
    pair_tokens = 2 * tokens
    width = n * g_hbm.shape[1]
    cols = g_hbm.shape[1]
    kept_dev = kept.shape[0] * kept.shape[1]
    levels = chips // 2
    side = lax.rem(chip, 2)
    level = lax.div(chip, 2)
    row_blocks = width // ROWBLK
    per_high = cols // ROWBLK
    q_pieces = q_box.shape[0]
    q_cols = q_box.shape[2]
    scale = width**-0.5
    mine = pl.ds(pl.multiple_of(core * tokens, tokens), tokens)

    def remote(src, dst, send, recv, device):
        return pltpu.make_async_remote_copy(
            src_ref=src, dst_ref=dst, send_sem=send, recv_sem=recv,
            device_id={"wide": device}, device_id_type=pl.DeviceIdType.MESH,
        )

    def grad_copy(source, device):
        rows = pl.ds(pl.multiple_of(device * tokens, tokens), tokens)
        half = pl.ds(pl.multiple_of(lax.rem(device, 2) * tokens, tokens), tokens)
        return remote(g_hbm.at[rows, :], gs.at[source, half, :], g_send.at[device], g_recv.at[source], device)

    def relay_copy(source):
        return remote(gs.at[source, mine, :], gs.at[source, mine, :], r_send.at[source], r_recv.at[source], partner)

    def kept_copy(source, device):
        return remote(kept, kb.at[source], k_send.at[device], k_recv.at[source], device)

    def target(to_level, to_side):
        return 4 * to_level + 2 * to_side + core

    def cross_copy(at):
        return remote(out_a.at[at], in_a.at[at], a_send.at[at], a_recv.at[at], target(level, 1 - side))

    def down_copy(source, at):
        return remote(out_b.at[at], in_b.at[source], b_send.at[at], b_recv.at[source], target(at, side))

    def score_copy(source, device):
        return remote(part, part_in.at[source], s_send.at[device], s_recv.at[source], device)

    x_local = pltpu.make_async_copy(x_hbm, xs.at[mine, :], own_sem.at[0])
    x_local.start()
    own_rows = pl.ds(pl.multiple_of(me * tokens, tokens), tokens)
    g_local = pltpu.make_async_copy(g_hbm.at[own_rows, :], gs.at[me, mine, :], own_sem.at[1])
    g_local.start()

    barrier = pltpu.get_barrier_semaphore()

    @pl.loop(1, n)
    def _(step):
        pl.semaphore_signal(
            barrier, inc=1, device_id={"wide": lax.rem(me + step, n)}, device_id_type=pl.DeviceIdType.MESH
        )

    pl.semaphore_wait(barrier, n - 1)

    x_pair = remote(x_hbm, xs.at[mine, :], x_sem.at[0], x_sem.at[1], partner)
    x_pair.start()

    @pl.loop(1, n)
    def _(step):
        grad_copy(me, lax.rem(me + step, n)).start()

    @pl.loop(1, chips)
    def _(step):
        kept_copy(me, lax.rem(me + 2 * step, n)).start()

    def query_copy(piece):
        begin = pl.multiple_of(piece * q_cols, q_cols)
        return pltpu.make_async_copy(q_hbm.at[:, pl.ds(begin, q_cols)], q_box.at[piece], q_sem.at[piece])

    @pl.loop(0, q_pieces)
    def _(piece):
        query_copy(piece).start()

    kb[me] = kept[...]
    table = signs(cols)

    def sign_row(signs_ref, block):
        per = cols // 128
        rows = [signs_ref[pl.ds(block * per + extra, 1), :] for extra in range(per)]
        return jnp.concatenate(rows, axis=1).astype(jnp.float32)

    def turn_block(block):
        lanes = pl.ds(pl.multiple_of(block * cols, cols), cols)
        signed = xs[:, lanes].astype(jnp.float32) * sign_row(column_sign, block)
        wide_f32[block] = jnp.dot(signed.astype(jnp.bfloat16), table, preferred_element_type=jnp.float32)

    g_local.wait()
    relay_copy(me).start()

    @pl.loop(1, n)
    def _(step):
        source = lax.rem(me + n - step, n)
        grad_copy(source, me).wait_recv()
        relay_copy(source).start()

        @pl.when(step == n // 2)
        def _():
            x_local.wait()
            x_pair.wait()

        @pl.when(step >= n // 2)
        def _():
            turn_block(2 * step - n)
            turn_block(2 * step - n + 1)

    @pl.loop(0, pair_tokens // 16)
    def _(tile):
        rows = pl.ds(pl.multiple_of(tile * 16, 16), 16)
        for lane in range(0, cols, 128):
            lanes = slice(lane, lane + 128)
            mixed = butterflies([wide_f32[block, rows, lanes] for block in range(n)])
            for block in range(n):
                turned[block, rows, lanes] = (mixed[block] * scale).astype(jnp.bfloat16)

    token_row = ids[:, pl.ds(pl.multiple_of(chip * pair_tokens, pair_tokens), pair_tokens)]
    weight = jnp.where(token_row != 0, scale, 0.0).astype(jnp.float32)

    for block in range(n):
        relay_copy(block).wait_recv()
        signed = (gs[block].astype(jnp.float32) * sign_row(row_sign, block)).astype(jnp.bfloat16)
        tall_f32[block] = lax.dot_general(
            table, signed, (((1,), (1,)), ((), ())), preferred_element_type=jnp.float32
        )

    @pl.loop(0, cols // 16)
    def _(tile):
        rows = pl.ds(pl.multiple_of(tile * 16, 16), 16)
        for lane in range(0, pair_tokens, 128):
            lanes = slice(lane, lane + 128)
            mixed = butterflies([tall_f32[block, rows, lanes] for block in range(n)])
            for block in range(n):
                begin = block * pair_tokens + lane
                left[rows, begin : begin + 128] = (mixed[block] * weight[:, lanes]).astype(jnp.bfloat16)

    def contribution(device):
        rows = kb[device]
        local = jnp.concatenate([rows[at : at + 1] for at in range(rows.shape[0])], axis=1)
        local = local - device * (cols * row_blocks)
        column = jnp.right_shift(local, row_blocks.bit_length() - 1)
        row = jnp.bitwise_and(local, row_blocks - 1)
        high = jnp.right_shift(row, per_high.bit_length() - 1)
        low = jnp.bitwise_and(row, per_high - 1)
        hit = lax.broadcasted_iota(jnp.int32, (cols, kept_dev), 0) == column
        chosen = jnp.dot(
            turned[device],
            jnp.where(hit, 1.0, 0.0).astype(jnp.bfloat16),
            preferred_element_type=jnp.float32,
        )
        for block in range(n):
            spread[block * pair_tokens : (block + 1) * pair_tokens, :] = jnp.where(high == block, chosen, 0.0).astype(
                jnp.bfloat16
            )
        full = jnp.dot(left[...], spread[...], preferred_element_type=jnp.float32)
        result = full[:ROWBLK]
        for block in range(1, per_high):
            result = jnp.where(low == block, full[block * ROWBLK : (block + 1) * ROWBLK], result)
        return result

    @pl.loop(0, levels + 1)
    def _(step):
        @pl.when(step < levels)
        def _():
            at = lax.rem(level + 1 + step, levels)
            device = target(at, 1 - side)
            kept_copy(device, me).wait_recv()
            out_a[at] = contribution(device).astype(jnp.bfloat16)
            cross_copy(at).start()

        @pl.when(step >= 1)
        def _():
            at = lax.rem(level + step, levels)
            device = target(at, side)

            @pl.when(step < levels)
            def _():
                kept_copy(device, me).wait_recv()

            total[...] = contribution(device)
            cross_copy(at).wait_recv()

            @pl.when(step < levels)
            def _():
                out_b[at] = (total[...] + in_a[at].astype(jnp.float32)).astype(jnp.bfloat16)
                down_copy(level, at).start()

    total[...] += in_a[level].astype(jnp.float32)

    @pl.loop(1, levels)
    def _(step):
        source = lax.rem(level + levels - step, levels)
        down_copy(source, level).wait_recv()
        total[...] += in_b[source].astype(jnp.float32)

    rounded = total[...].T.astype(jnp.bfloat16)
    sk_ref[...] = rounded
    skf[...] = rounded.astype(jnp.float32)
    blocks_piece = q_cols // ROWBLK
    group = 4

    def piece_scores(piece, acc):
        query_copy(piece).wait()

        def body(index, acc):
            for extra in range(group):
                block = (index * group + extra) * 2
                lanes = pl.ds(pl.multiple_of(block * ROWBLK, 2 * ROWBLK), 2 * ROWBLK)
                line = [
                    jnp.broadcast_to(skf[pl.ds(piece * blocks_piece + block + at, 1), :], (16, ROWBLK))
                    for at in range(2)
                ]
                acc = acc + lax.dot_general(
                    jnp.concatenate(line, axis=1).astype(jnp.bfloat16),
                    q_box[piece, :, lanes],
                    (((1,), (1,)), ((), ())),
                    preferred_element_type=jnp.float32,
                )
            return acc

        return lax.fori_loop(0, blocks_piece // (2 * group), body, acc)

    nq = q_hbm.shape[0]
    acc = lax.fori_loop(0, q_pieces, piece_scores, jnp.zeros((16, nq), jnp.float32))
    part[...] = acc[:8]

    @pl.loop(1, n)
    def _(step):
        score_copy(me, lax.rem(me + step, n)).start()

    part_in[me] = acc[:8]

    @pl.loop(1, n)
    def _(step):
        score_copy(lax.rem(me + step, n), me).wait_recv()

    summed = part_in[0]
    for block in range(1, n):
        summed = summed + part_in[block]
    count = score_ref.shape[0]
    spot = lax.broadcasted_iota(jnp.int32, (count, nq), 0) + me * count
    own = lax.broadcasted_iota(jnp.int32, (count, nq), 1) == spot
    score_ref[...] = jnp.sum(jnp.where(own, summed[:1], 0.0), axis=1, keepdims=True)

    @pl.loop(1, n)
    def _(step):
        device = lax.rem(me + step, n)
        grad_copy(me, device).wait_send()
        score_copy(me, device).wait_send()

    @pl.loop(0, n)
    def _(step):
        relay_copy(step).wait_send()

    @pl.loop(1, chips)
    def _(step):
        kept_copy(me, lax.rem(me + 2 * step, n)).wait_send()

    @pl.loop(0, levels)
    def _(step):
        cross_copy(step).wait_send()

    @pl.loop(1, levels)
    def _(step):
        down_copy(level, lax.rem(level + step, levels)).wait_send()


def per_device(n, activations, output_grads, token_ids, row_signs, column_signs, kept_blocks, queries):
    items, tokens, width = activations.shape
    cols = output_grads.shape[2]
    kept_dev = kept_blocks.shape[0]
    nq = queries.shape[0]
    q_pieces = 8
    fits = (
        items == 1
        and n % 4 == 0
        and n & (n - 1) == 0
        and cols & (cols - 1) == 0
        and cols % ROWBLK == 0
        and tokens % 16 == 0
        and (2 * tokens) % 128 == 0
        and kept_dev % 128 == 0
        and nq % (8 * n) == 0
        and nq % 64 == 0
        and kept_dev % (8 * q_pieces) == 0
        and queries.size * 2 <= 2**25
    )
    if not fits:
        return per_device_plain(
            activations, output_grads, token_ids, row_signs, column_signs, kept_blocks, queries
        )
    chips = n // 2
    bf16, f32 = jnp.bfloat16, jnp.float32
    dma = pltpu.SemaphoreType.DMA
    any_spec = pl.BlockSpec(memory_space=pl.ANY)
    vmem_spec = pl.BlockSpec(memory_space=pltpu.VMEM)
    sketches, scores = pl.pallas_call(
        functools.partial(kernel, n),
        out_shape=(
            jax.ShapeDtypeStruct((kept_dev, ROWBLK), bf16),
            jax.ShapeDtypeStruct((nq // n, 1), f32),
        ),
        in_specs=[any_spec, any_spec, vmem_spec, vmem_spec, vmem_spec, vmem_spec, any_spec],
        out_specs=(vmem_spec, vmem_spec),
        scratch_shapes=[
            pltpu.VMEM((2 * tokens, width), bf16),
            pltpu.VMEM((n, 2 * tokens, cols), bf16),
            pltpu.VMEM((n, kept_dev // 128, 128), jnp.int32),
            pltpu.VMEM((n, 2 * tokens, cols), f32),
            pltpu.VMEM((n, cols, 2 * tokens), f32),
            pltpu.VMEM((n, 2 * tokens, cols), bf16),
            pltpu.VMEM((cols, n * 2 * tokens), bf16),
            pltpu.VMEM((n * 2 * tokens, kept_dev), bf16),
            pltpu.VMEM((chips // 2, ROWBLK, kept_dev), bf16),
            pltpu.VMEM((chips // 2, ROWBLK, kept_dev), bf16),
            pltpu.VMEM((chips // 2, ROWBLK, kept_dev), bf16),
            pltpu.VMEM((chips // 2, ROWBLK, kept_dev), bf16),
            pltpu.VMEM((ROWBLK, kept_dev), f32),
            pltpu.VMEM((q_pieces, nq, queries.shape[1] // q_pieces), bf16),
            pltpu.VMEM((kept_dev, ROWBLK), f32),
            pltpu.VMEM((8, nq), f32),
            pltpu.VMEM((n, 8, nq), f32),
            dma((2,)), dma((2,)), dma((q_pieces,)),
            dma((n,)), dma((n,)), dma((n,)), dma((n,)), dma((n,)), dma((n,)),
            dma((chips // 2,)), dma((chips // 2,)), dma((chips // 2,)), dma((chips // 2,)), dma((n,)), dma((n,)),
        ],
        compiler_params=pltpu.CompilerParams(
            collective_id=0, has_side_effects=True, vmem_limit_bytes=60 * 2**20
        ),
    )(
        activations[0],
        output_grads[0],
        token_ids,
        column_signs.reshape(-1, 128),
        row_signs.reshape(-1, 128),
        kept_blocks.reshape(-1, 128),
        queries,
    )
    return sketches.reshape(1, kept_dev * ROWBLK), scores


def solution(mesh):
    placed = (
        P("grp", "wide", None),
        P("grp", None, "wide"),
        P("grp", None),
        P(),
        P(),
        P("wide"),
        P(None, "wide"),
    )
    return jax.shard_map(
        functools.partial(per_device, mesh.shape["wide"]),
        mesh=mesh,
        in_specs=placed,
        out_specs=(P("grp", "wide"), P("wide", "grp")),
        check_vma=False,
    )
```

```python
import functools

import jax
import jax.numpy as jnp
from jax import lax
from jax.experimental import pallas as pl
from jax.experimental.pallas import tpu as pltpu
from jax.sharding import PartitionSpec as P

ROWBLK = 128


def sign_table(bit_count):
    length = 2**bit_count
    indices = jnp.arange(length, dtype=jnp.int32)
    common = jnp.bitwise_and(indices[:, None], indices[None, :])
    parity = jnp.zeros((length, length), jnp.int32)
    for position in range(bit_count):
        parity = parity + jnp.bitwise_and(jnp.right_shift(common, position), 1)
    signs = 1 - 2 * jnp.bitwise_and(parity, 1)
    return (signs.astype(jnp.float32) * length ** (-0.5)).astype(jnp.bfloat16)


def hadamard_table(order_size):
    total_bits = order_size.bit_length() - 1
    low_bits = total_bits // 2
    high_table = sign_table(total_bits - low_bits)
    low_table = sign_table(low_bits)
    high_table, low_table = lax.optimization_barrier((high_table, low_table))
    return (high_table[:, None, :, None] * low_table[None, :, None, :]).reshape(
        order_size, order_size
    )


def per_device_plain(activations, output_grads, token_ids, row_signs, column_signs, kept_blocks, queries):
    model_width = column_signs.shape[0]
    hadamard = hadamard_table(model_width)
    row_blocks = model_width // ROWBLK
    column_sign = column_signs.astype(jnp.bfloat16)
    row_sign = row_signs.astype(jnp.bfloat16)
    weight = (token_ids != 0).astype(jnp.bfloat16)
    columns_dev = output_grads.shape[2]
    device = lax.axis_index("wide")
    local_blocks = kept_blocks - device * (columns_dev * row_blocks)
    turned = jnp.einsum(
        "stj,jk->stk",
        activations * column_sign[None, None, :],
        hadamard,
        preferred_element_type=jnp.float32,
    ).astype(jnp.bfloat16)
    columns = lax.all_to_all(turned, "wide", split_axis=2, concat_axis=1, tiled=True)
    weighted = columns * weight[:, :, None]
    half_turned = jnp.einsum(
        "stc,sti->sci",
        weighted,
        lax.all_gather(output_grads, "wide", axis=2, tiled=True),
        preferred_element_type=jnp.float32,
    ).astype(jnp.bfloat16)
    signed = half_turned * row_sign[None, None, :]
    projected = jnp.einsum("scj,ji->sci", signed, hadamard, preferred_element_type=jnp.float32)
    items = projected.shape[0]
    block_rows = projected.reshape(items, projected.shape[1] * row_blocks, ROWBLK)
    picked = jnp.take(block_rows, local_blocks, axis=1)
    sketches = picked.reshape(items, picked.shape[1] * ROWBLK).astype(jnp.bfloat16)
    scores = lax.psum_scatter(
        jnp.einsum("qc,sc->qs", queries, sketches, preferred_element_type=jnp.float32),
        "wide",
        scatter_dimension=0,
        tiled=True,
    )
    return (sketches, scores)


def signs(size):
    common = jnp.bitwise_and(
        lax.broadcasted_iota(jnp.int32, (size, size), 0),
        lax.broadcasted_iota(jnp.int32, (size, size), 1),
    )
    shift = 1
    while shift < size:
        common = jnp.bitwise_xor(common, jnp.right_shift(common, shift))
        shift *= 2
    return (1 - 2 * jnp.bitwise_and(common, 1)).astype(jnp.float32).astype(jnp.bfloat16)


def butterflies(values):
    values = list(values)
    step = 1
    while step < len(values):
        for low in range(len(values)):
            if low & step == 0:
                first, second = values[low], values[low + step]
                values[low], values[low + step] = first + second, first - second
        step *= 2
    return values


def kernel(
    n, x_hbm, g_hbm, ids, column_sign, row_sign, kept, q_hbm,
    sk_ref, score_ref,
    xs, gs, kb, wide_f32, tall_f32, turned, left, spread, out_a, in_a, out_b, in_b, total, q_box, skf, part, part_in,
    x_sem, own_sem, q_sem, g_send, g_recv, r_send, r_recv, k_send, k_recv, a_send, a_recv, b_send, b_recv, s_send, s_recv,
):
    me = lax.axis_index("wide")
    core = lax.rem(me, 2)
    chip = lax.div(me, 2)
    partner = me + 1 - 2 * core
    chips = n // 2
    tokens = x_hbm.shape[0]
    pair_tokens = 2 * tokens
    width = n * g_hbm.shape[1]
    cols = g_hbm.shape[1]
    kept_dev = kept.shape[0] * kept.shape[1]
    levels = chips // 2
    side = lax.rem(chip, 2)
    level = lax.div(chip, 2)
    row_blocks = width // ROWBLK
    per_high = cols // ROWBLK
    q_pieces = q_box.shape[0]
    q_cols = q_box.shape[2]
    scale = width**-0.5
    mine = pl.ds(pl.multiple_of(core * tokens, tokens), tokens)

    def remote(src, dst, send, recv, device):
        return pltpu.make_async_remote_copy(
            src_ref=src, dst_ref=dst, send_sem=send, recv_sem=recv,
            device_id={"wide": device}, device_id_type=pl.DeviceIdType.MESH,
        )

    def grad_copy(source, device):
        rows = pl.ds(pl.multiple_of(device * tokens, tokens), tokens)
        half = pl.ds(pl.multiple_of(lax.rem(device, 2) * tokens, tokens), tokens)
        return remote(g_hbm.at[rows, :], gs.at[source, half, :], g_send.at[device], g_recv.at[source], device)

    def relay_copy(source):
        return remote(gs.at[source, mine, :], gs.at[source, mine, :], r_send.at[source], r_recv.at[source], partner)

    def kept_copy(source, device):
        return remote(kept, kb.at[source], k_send.at[device], k_recv.at[source], device)

    def target(to_level, to_side):
        return 4 * to_level + 2 * to_side + core

    def cross_copy(at):
        return remote(out_a.at[at], in_a.at[at], a_send.at[at], a_recv.at[at], target(level, 1 - side))

    def down_copy(source, at):
        return remote(out_b.at[at], in_b.at[source], b_send.at[at], b_recv.at[source], target(at, side))

    def score_copy(source, device):
        return remote(part, part_in.at[source], s_send.at[device], s_recv.at[source], device)

    x_local = pltpu.make_async_copy(x_hbm, xs.at[mine, :], own_sem.at[0])
    x_local.start()
    own_rows = pl.ds(pl.multiple_of(me * tokens, tokens), tokens)
    g_local = pltpu.make_async_copy(g_hbm.at[own_rows, :], gs.at[me, mine, :], own_sem.at[1])
    g_local.start()

    barrier = pltpu.get_barrier_semaphore()

    @pl.loop(1, n)
    def _(step):
        pl.semaphore_signal(
            barrier, inc=1, device_id={"wide": lax.rem(me + step, n)}, device_id_type=pl.DeviceIdType.MESH
        )

    pl.semaphore_wait(barrier, n - 1)

    x_pair = remote(x_hbm, xs.at[mine, :], x_sem.at[0], x_sem.at[1], partner)
    x_pair.start()

    @pl.loop(1, n)
    def _(step):
        grad_copy(me, lax.rem(me + step, n)).start()

    @pl.loop(1, chips)
    def _(step):
        kept_copy(me, lax.rem(me + 2 * step, n)).start()

    def query_copy(piece):
        begin = pl.multiple_of(piece * q_cols, q_cols)
        return pltpu.make_async_copy(q_hbm.at[:, pl.ds(begin, q_cols)], q_box.at[piece], q_sem.at[piece])

    @pl.loop(0, q_pieces)
    def _(piece):
        query_copy(piece).start()

    kb[me] = kept[...]
    table = signs(cols)

    def sign_row(signs_ref, block):
        per = cols // 128
        rows = [signs_ref[pl.ds(block * per + extra, 1), :] for extra in range(per)]
        return jnp.concatenate(rows, axis=1).astype(jnp.float32)

    def turn_block(block):
        lanes = pl.ds(pl.multiple_of(block * cols, cols), cols)
        signed = xs[:, lanes].astype(jnp.float32) * sign_row(column_sign, block)
        wide_f32[block] = jnp.dot(signed.astype(jnp.bfloat16), table, preferred_element_type=jnp.float32)

    g_local.wait()
    relay_copy(me).start()

    @pl.loop(1, n)
    def _(step):
        source = lax.rem(me + n - step, n)
        grad_copy(source, me).wait_recv()
        relay_copy(source).start()

        @pl.when(step == n // 2)
        def _():
            x_local.wait()
            x_pair.wait()

        @pl.when(step >= n // 2)
        def _():
            turn_block(2 * step - n)
            turn_block(2 * step - n + 1)

    @pl.loop(0, pair_tokens // 16)
    def _(tile):
        rows = pl.ds(pl.multiple_of(tile * 16, 16), 16)
        for lane in range(0, cols, 128):
            lanes = slice(lane, lane + 128)
            mixed = butterflies([wide_f32[block, rows, lanes] for block in range(n)])
            for block in range(n):
                turned[block, rows, lanes] = (mixed[block] * scale).astype(jnp.bfloat16)

    token_row = ids[:, pl.ds(pl.multiple_of(chip * pair_tokens, pair_tokens), pair_tokens)]
    weight = jnp.where(token_row != 0, scale, 0.0).astype(jnp.float32)

    for block in range(n):
        relay_copy(block).wait_recv()
        signed = (gs[block].astype(jnp.float32) * sign_row(row_sign, block)).astype(jnp.bfloat16)
        tall_f32[block] = lax.dot_general(
            table, signed, (((1,), (1,)), ((), ())), preferred_element_type=jnp.float32
        )

    @pl.loop(0, cols // 16)
    def _(tile):
        rows = pl.ds(pl.multiple_of(tile * 16, 16), 16)
        for lane in range(0, pair_tokens, 128):
            lanes = slice(lane, lane + 128)
            mixed = butterflies([tall_f32[block, rows, lanes] for block in range(n)])
            for block in range(n):
                begin = block * pair_tokens + lane
                left[rows, begin : begin + 128] = (mixed[block] * weight[:, lanes]).astype(jnp.bfloat16)

    def contribution(device):
        rows = kb[device]
        local = jnp.concatenate([rows[at : at + 1] for at in range(rows.shape[0])], axis=1)
        local = local - device * (cols * row_blocks)
        column = jnp.right_shift(local, row_blocks.bit_length() - 1)
        row = jnp.bitwise_and(local, row_blocks - 1)
        high = jnp.right_shift(row, per_high.bit_length() - 1)
        low = jnp.bitwise_and(row, per_high - 1)
        hit = lax.broadcasted_iota(jnp.int32, (cols, kept_dev), 0) == column
        chosen = jnp.dot(
            turned[device],
            jnp.where(hit, 1.0, 0.0).astype(jnp.bfloat16),
            preferred_element_type=jnp.float32,
        )
        for block in range(n):
            spread[block * pair_tokens : (block + 1) * pair_tokens, :] = jnp.where(high == block, chosen, 0.0).astype(
                jnp.bfloat16
            )
        full = jnp.dot(left[...], spread[...], preferred_element_type=jnp.float32)
        result = full[:ROWBLK]
        for block in range(1, per_high):
            result = jnp.where(low == block, full[block * ROWBLK : (block + 1) * ROWBLK], result)
        return result

    @pl.loop(0, levels + 1)
    def _(step):
        @pl.when(step < levels)
        def _():
            at = lax.rem(level + 1 + step, levels)
            device = target(at, 1 - side)
            kept_copy(device, me).wait_recv()
            out_a[at] = contribution(device).astype(jnp.bfloat16)
            cross_copy(at).start()

        @pl.when(step >= 1)
        def _():
            at = lax.rem(level + step, levels)
            device = target(at, side)

            @pl.when(step < levels)
            def _():
                kept_copy(device, me).wait_recv()

            total[...] = contribution(device)
            cross_copy(at).wait_recv()

            @pl.when(step < levels)
            def _():
                out_b[at] = (total[...] + in_a[at].astype(jnp.float32)).astype(jnp.bfloat16)
                down_copy(level, at).start()

    total[...] += in_a[level].astype(jnp.float32)

    @pl.loop(1, levels)
    def _(step):
        source = lax.rem(level + levels - step, levels)
        down_copy(source, level).wait_recv()
        total[...] += in_b[source].astype(jnp.float32)

    rounded = total[...].T.astype(jnp.bfloat16)
    sk_ref[...] = rounded
    skf[...] = rounded.astype(jnp.float32)
    blocks_piece = q_cols // ROWBLK
    nq = q_hbm.shape[0]

    def line_of(piece, block):
        line = skf[pl.ds(piece * blocks_piece + block, 1), :]
        return jnp.broadcast_to(line, (16, ROWBLK))[None]

    def piece_scores(piece, accs):
        query_copy(piece).wait()

        def body(index, accs):
            accs = list(accs)
            for extra in range(4):
                block = (index * 4 + extra) * 2
                lines = [line_of(piece, block + at) for at in range(2)]
                for top in range(0, nq, 64):
                    both = None
                    for at in range(2):
                        lanes = pl.ds(pl.multiple_of((block + at) * ROWBLK, ROWBLK), ROWBLK)
                        rows = q_box[piece, top : top + 64, lanes].reshape(64 // 16, 16, ROWBLK)
                        term = rows.astype(jnp.float32) * lines[at]
                        both = term if both is None else both + term
                    accs[top // 64] += both.reshape(64, ROWBLK).astype(jnp.float32)
            return tuple(accs)

        return lax.fori_loop(0, blocks_piece // (2 * 4), body, accs)

    zeros = tuple(jnp.zeros((64, ROWBLK), jnp.float32) for _ in range(nq // 64))
    accs = lax.fori_loop(0, q_pieces, piece_scores, zeros)
    columns = jnp.concatenate(accs, axis=0).T
    part[...] = jnp.sum(columns, axis=0, keepdims=True)

    @pl.loop(1, n)
    def _(step):
        score_copy(me, lax.rem(me + step, n)).start()

    part_in[me] = part[...]

    @pl.loop(1, n)
    def _(step):
        score_copy(lax.rem(me + step, n), me).wait_recv()

    summed = part_in[0]
    for block in range(1, n):
        summed = summed + part_in[block]
    count = score_ref.shape[1]
    spot = lax.broadcasted_iota(jnp.int32, (128, nq), 0) + me * count
    own = lax.broadcasted_iota(jnp.int32, (128, nq), 1) == spot
    column = jnp.sum(jnp.where(own, summed, 0.0), axis=1, keepdims=True)
    score_ref[...] = jnp.broadcast_to(column, (128, 128)).T[:1, :count]

    @pl.loop(1, n)
    def _(step):
        device = lax.rem(me + step, n)
        grad_copy(me, device).wait_send()
        score_copy(me, device).wait_send()

    @pl.loop(0, n)
    def _(step):
        relay_copy(step).wait_send()

    @pl.loop(1, chips)
    def _(step):
        kept_copy(me, lax.rem(me + 2 * step, n)).wait_send()

    @pl.loop(0, levels)
    def _(step):
        cross_copy(step).wait_send()

    @pl.loop(1, levels)
    def _(step):
        down_copy(level, lax.rem(level + step, levels)).wait_send()


def per_device(n, activations, output_grads, token_ids, row_signs, column_signs, kept_blocks, queries):
    items, tokens, width = activations.shape
    cols = output_grads.shape[2]
    kept_dev = kept_blocks.shape[0]
    nq = queries.shape[0]
    q_pieces = 8
    fits = (
        items == 1
        and n % 4 == 0
        and n & (n - 1) == 0
        and cols & (cols - 1) == 0
        and cols % ROWBLK == 0
        and tokens % 16 == 0
        and (2 * tokens) % 128 == 0
        and kept_dev % 128 == 0
        and nq % (8 * n) == 0
        and nq % 64 == 0
        and nq // n <= 128
        and kept_dev % (8 * q_pieces) == 0
        and queries.size * 2 <= 2**25
    )
    if not fits:
        return per_device_plain(
            activations, output_grads, token_ids, row_signs, column_signs, kept_blocks, queries
        )
    chips = n // 2
    bf16, f32 = jnp.bfloat16, jnp.float32
    dma = pltpu.SemaphoreType.DMA
    any_spec = pl.BlockSpec(memory_space=pl.ANY)
    vmem_spec = pl.BlockSpec(memory_space=pltpu.VMEM)
    sketches, scores = pl.pallas_call(
        functools.partial(kernel, n),
        out_shape=(
            jax.ShapeDtypeStruct((kept_dev, ROWBLK), bf16),
            jax.ShapeDtypeStruct((1, nq // n), f32),
        ),
        in_specs=[any_spec, any_spec, vmem_spec, vmem_spec, vmem_spec, vmem_spec, any_spec],
        out_specs=(vmem_spec, vmem_spec),
        scratch_shapes=[
            pltpu.VMEM((2 * tokens, width), bf16),
            pltpu.VMEM((n, 2 * tokens, cols), bf16),
            pltpu.VMEM((n, kept_dev // 128, 128), jnp.int32),
            pltpu.VMEM((n, 2 * tokens, cols), f32),
            pltpu.VMEM((n, cols, 2 * tokens), f32),
            pltpu.VMEM((n, 2 * tokens, cols), bf16),
            pltpu.VMEM((cols, n * 2 * tokens), bf16),
            pltpu.VMEM((n * 2 * tokens, kept_dev), bf16),
            pltpu.VMEM((chips // 2, ROWBLK, kept_dev), bf16),
            pltpu.VMEM((chips // 2, ROWBLK, kept_dev), bf16),
            pltpu.VMEM((chips // 2, ROWBLK, kept_dev), bf16),
            pltpu.VMEM((chips // 2, ROWBLK, kept_dev), bf16),
            pltpu.VMEM((ROWBLK, kept_dev), f32),
            pltpu.VMEM((q_pieces, nq, queries.shape[1] // q_pieces), bf16),
            pltpu.VMEM((kept_dev, ROWBLK), f32),
            pltpu.VMEM((1, nq), f32),
            pltpu.VMEM((n, 1, nq), f32),
            dma((2,)), dma((2,)), dma((q_pieces,)),
            dma((n,)), dma((n,)), dma((n,)), dma((n,)), dma((n,)), dma((n,)),
            dma((chips // 2,)), dma((chips // 2,)), dma((chips // 2,)), dma((chips // 2,)), dma((n,)), dma((n,)),
        ],
        compiler_params=pltpu.CompilerParams(
            collective_id=0, has_side_effects=True, vmem_limit_bytes=60 * 2**20
        ),
    )(
        activations[0],
        output_grads[0],
        token_ids,
        column_signs.reshape(-1, 128),
        row_signs.reshape(-1, 128),
        kept_blocks.reshape(-1, 128),
        queries,
    )
    return sketches.reshape(1, kept_dev * ROWBLK), scores.reshape(nq // n, 1)


def solution(mesh):
    placed = (
        P("grp", "wide", None),
        P("grp", None, "wide"),
        P("grp", None),
        P(),
        P(),
        P("wide"),
        P(None, "wide"),
    )
    return jax.shard_map(
        functools.partial(per_device, mesh.shape["wide"]),
        mesh=mesh,
        in_specs=placed,
        out_specs=(P("grp", "wide"), P("wide", "grp")),
        check_vma=False,
    )
```

```python
import functools

import jax
import jax.numpy as jnp
from jax import lax
from jax.experimental import pallas as pl
from jax.experimental.pallas import tpu as pltpu
from jax.sharding import PartitionSpec as P

ROWBLK = 128


def sign_table(bit_count):
    length = 2**bit_count
    indices = jnp.arange(length, dtype=jnp.int32)
    common = jnp.bitwise_and(indices[:, None], indices[None, :])
    parity = jnp.zeros((length, length), jnp.int32)
    for position in range(bit_count):
        parity = parity + jnp.bitwise_and(jnp.right_shift(common, position), 1)
    signs = 1 - 2 * jnp.bitwise_and(parity, 1)
    return (signs.astype(jnp.float32) * length ** (-0.5)).astype(jnp.bfloat16)


def hadamard_table(order_size):
    total_bits = order_size.bit_length() - 1
    low_bits = total_bits // 2
    high_table = sign_table(total_bits - low_bits)
    low_table = sign_table(low_bits)
    high_table, low_table = lax.optimization_barrier((high_table, low_table))
    return (high_table[:, None, :, None] * low_table[None, :, None, :]).reshape(
        order_size, order_size
    )


def per_device_plain(activations, output_grads, token_ids, row_signs, column_signs, kept_blocks, queries):
    model_width = column_signs.shape[0]
    hadamard = hadamard_table(model_width)
    row_blocks = model_width // ROWBLK
    column_sign = column_signs.astype(jnp.bfloat16)
    row_sign = row_signs.astype(jnp.bfloat16)
    weight = (token_ids != 0).astype(jnp.bfloat16)
    columns_dev = output_grads.shape[2]
    device = lax.axis_index("wide")
    local_blocks = kept_blocks - device * (columns_dev * row_blocks)
    turned = jnp.einsum(
        "stj,jk->stk",
        activations * column_sign[None, None, :],
        hadamard,
        preferred_element_type=jnp.float32,
    ).astype(jnp.bfloat16)
    columns = lax.all_to_all(turned, "wide", split_axis=2, concat_axis=1, tiled=True)
    weighted = columns * weight[:, :, None]
    half_turned = jnp.einsum(
        "stc,sti->sci",
        weighted,
        lax.all_gather(output_grads, "wide", axis=2, tiled=True),
        preferred_element_type=jnp.float32,
    ).astype(jnp.bfloat16)
    signed = half_turned * row_sign[None, None, :]
    projected = jnp.einsum("scj,ji->sci", signed, hadamard, preferred_element_type=jnp.float32)
    items = projected.shape[0]
    block_rows = projected.reshape(items, projected.shape[1] * row_blocks, ROWBLK)
    picked = jnp.take(block_rows, local_blocks, axis=1)
    sketches = picked.reshape(items, picked.shape[1] * ROWBLK).astype(jnp.bfloat16)
    scores = lax.psum_scatter(
        jnp.einsum("qc,sc->qs", queries, sketches, preferred_element_type=jnp.float32),
        "wide",
        scatter_dimension=0,
        tiled=True,
    )
    return (sketches, scores)


def signs(size):
    common = jnp.bitwise_and(
        lax.broadcasted_iota(jnp.int32, (size, size), 0),
        lax.broadcasted_iota(jnp.int32, (size, size), 1),
    )
    shift = 1
    while shift < size:
        common = jnp.bitwise_xor(common, jnp.right_shift(common, shift))
        shift *= 2
    return (1 - 2 * jnp.bitwise_and(common, 1)).astype(jnp.float32).astype(jnp.bfloat16)


def butterflies(values):
    values = list(values)
    step = 1
    while step < len(values):
        for low in range(len(values)):
            if low & step == 0:
                first, second = values[low], values[low + step]
                values[low], values[low + step] = first + second, first - second
        step *= 2
    return values


def kernel(
    n, x_hbm, g_hbm, ids, column_sign, row_sign, kept, q_hbm,
    sk_ref, score_ref,
    xs, gs, kb, wide_f32, tall_f32, turned, left, spread, out_a, in_a, out_b, in_b, total, q_box, skf, part, part_in,
    x_sem, own_sem, q_sem, g_send, g_recv, r_send, r_recv, k_send, k_recv, a_send, a_recv, b_send, b_recv, s_send, s_recv,
):
    me = lax.axis_index("wide")
    core = lax.rem(me, 2)
    chip = lax.div(me, 2)
    partner = me + 1 - 2 * core
    chips = n // 2
    tokens = x_hbm.shape[0]
    pair_tokens = 2 * tokens
    width = n * g_hbm.shape[1]
    cols = g_hbm.shape[1]
    kept_dev = kept.shape[0] * kept.shape[1]
    levels = chips // 2
    side = lax.rem(chip, 2)
    level = lax.div(chip, 2)
    row_blocks = width // ROWBLK
    per_high = cols // ROWBLK
    q_pieces = q_box.shape[0]
    q_cols = q_box.shape[2]
    scale = width**-0.5
    mine = pl.ds(pl.multiple_of(core * tokens, tokens), tokens)

    def remote(src, dst, send, recv, device):
        return pltpu.make_async_remote_copy(
            src_ref=src, dst_ref=dst, send_sem=send, recv_sem=recv,
            device_id={"wide": device}, device_id_type=pl.DeviceIdType.MESH,
        )

    def grad_copy(source, device):
        rows = pl.ds(pl.multiple_of(device * tokens, tokens), tokens)
        half = pl.ds(pl.multiple_of(lax.rem(device, 2) * tokens, tokens), tokens)
        return remote(g_hbm.at[rows, :], gs.at[source, half, :], g_send.at[device], g_recv.at[source], device)

    def relay_copy(source):
        return remote(gs.at[source, mine, :], gs.at[source, mine, :], r_send.at[source], r_recv.at[source], partner)

    def kept_copy(source, device):
        return remote(kept, kb.at[source], k_send.at[device], k_recv.at[source], device)

    def target(to_level, to_side):
        return 4 * to_level + 2 * to_side + core

    def cross_copy(at):
        return remote(out_a.at[at], in_a.at[at], a_send.at[at], a_recv.at[at], target(level, 1 - side))

    def down_copy(source, at):
        return remote(out_b.at[at], in_b.at[source], b_send.at[at], b_recv.at[source], target(at, side))

    def score_copy(source, device):
        return remote(part, part_in.at[source], s_send.at[device], s_recv.at[source], device)

    x_local = pltpu.make_async_copy(x_hbm, xs.at[mine, :], own_sem.at[0])
    x_local.start()
    own_rows = pl.ds(pl.multiple_of(me * tokens, tokens), tokens)
    g_local = pltpu.make_async_copy(g_hbm.at[own_rows, :], gs.at[me, mine, :], own_sem.at[1])
    g_local.start()

    barrier = pltpu.get_barrier_semaphore()

    @pl.loop(1, n)
    def _(step):
        pl.semaphore_signal(
            barrier, inc=1, device_id={"wide": lax.rem(me + step, n)}, device_id_type=pl.DeviceIdType.MESH
        )

    pl.semaphore_wait(barrier, n - 1)

    x_pair = remote(x_hbm, xs.at[mine, :], x_sem.at[0], x_sem.at[1], partner)
    x_pair.start()

    @pl.loop(1, n)
    def _(step):
        grad_copy(me, lax.rem(me + step, n)).start()

    @pl.loop(1, chips)
    def _(step):
        kept_copy(me, lax.rem(me + 2 * step, n)).start()

    def query_copy(piece):
        begin = pl.multiple_of(piece * q_cols, q_cols)
        return pltpu.make_async_copy(q_hbm.at[:, pl.ds(begin, q_cols)], q_box.at[piece], q_sem.at[piece])

    @pl.loop(0, q_pieces)
    def _(piece):
        query_copy(piece).start()

    kb[me] = kept[...]
    table = signs(cols)

    def sign_row(signs_ref, block):
        per = cols // 128
        rows = [signs_ref[pl.ds(block * per + extra, 1), :] for extra in range(per)]
        return jnp.concatenate(rows, axis=1).astype(jnp.float32).astype(jnp.bfloat16)

    def turn_block(block):
        lanes = pl.ds(pl.multiple_of(block * cols, cols), cols)
        signed = xs[:, lanes] * sign_row(column_sign, block)
        wide_f32[block] = jnp.dot(signed, table, preferred_element_type=jnp.float32)

    g_local.wait()
    relay_copy(me).start()

    @pl.loop(1, n)
    def _(step):
        source = lax.rem(me + n - step, n)
        grad_copy(source, me).wait_recv()
        relay_copy(source).start()

        @pl.when(step == n // 2)
        def _():
            x_local.wait()
            x_pair.wait()

        @pl.when(step >= n // 2)
        def _():
            turn_block(2 * step - n)
            turn_block(2 * step - n + 1)

    @pl.loop(0, pair_tokens // 16)
    def _(tile):
        rows = pl.ds(pl.multiple_of(tile * 16, 16), 16)
        for lane in range(0, cols, 128):
            lanes = slice(lane, lane + 128)
            mixed = butterflies([wide_f32[block, rows, lanes] for block in range(n)])
            for block in range(n):
                turned[block, rows, lanes] = (mixed[block] * scale).astype(jnp.bfloat16)

    token_row = ids[:, pl.ds(pl.multiple_of(chip * pair_tokens, pair_tokens), pair_tokens)]
    weight = jnp.where(token_row != 0, scale, 0.0).astype(jnp.float32)

    for block in range(n):
        relay_copy(block).wait_recv()
        signed = gs[block] * sign_row(row_sign, block)
        tall_f32[block] = lax.dot_general(
            table, signed, (((1,), (1,)), ((), ())), preferred_element_type=jnp.float32
        )

    @pl.loop(0, cols // 16)
    def _(tile):
        rows = pl.ds(pl.multiple_of(tile * 16, 16), 16)
        for lane in range(0, pair_tokens, 128):
            lanes = slice(lane, lane + 128)
            mixed = butterflies([tall_f32[block, rows, lanes] for block in range(n)])
            for block in range(n):
                begin = block * pair_tokens + lane
                left[rows, begin : begin + 128] = (mixed[block] * weight[:, lanes]).astype(jnp.bfloat16)

    def contribution(device):
        rows = kb[device]
        local = jnp.concatenate([rows[at : at + 1] for at in range(rows.shape[0])], axis=1)
        local = local - device * (cols * row_blocks)
        column = jnp.right_shift(local, row_blocks.bit_length() - 1)
        row = jnp.bitwise_and(local, row_blocks - 1)
        high = jnp.right_shift(row, per_high.bit_length() - 1)
        low = jnp.bitwise_and(row, per_high - 1)
        hit = lax.broadcasted_iota(jnp.int32, (cols, kept_dev), 0) == column
        chosen = jnp.dot(
            turned[device],
            jnp.where(hit, 1.0, 0.0).astype(jnp.bfloat16),
            preferred_element_type=jnp.float32,
        )
        chosen = chosen.astype(jnp.bfloat16)
        for block in range(n):
            keep = jnp.where(high == block, 1.0, 0.0).astype(jnp.bfloat16)
            spread[block * pair_tokens : (block + 1) * pair_tokens, :] = chosen * keep
        full = jnp.dot(left[...], spread[...], preferred_element_type=jnp.float32)
        result = full[:ROWBLK]
        for block in range(1, per_high):
            result = jnp.where(low == block, full[block * ROWBLK : (block + 1) * ROWBLK], result)
        return result

    @pl.loop(0, levels + 1)
    def _(step):
        @pl.when(step < levels)
        def _():
            at = lax.rem(level + 1 + step, levels)
            device = target(at, 1 - side)
            kept_copy(device, me).wait_recv()
            out_a[at] = contribution(device).astype(jnp.bfloat16)
            cross_copy(at).start()

        @pl.when(step >= 1)
        def _():
            at = lax.rem(level + step, levels)
            device = target(at, side)

            @pl.when(step < levels)
            def _():
                kept_copy(device, me).wait_recv()

            total[...] = contribution(device)
            cross_copy(at).wait_recv()

            @pl.when(step < levels)
            def _():
                out_b[at] = (total[...] + in_a[at].astype(jnp.float32)).astype(jnp.bfloat16)
                down_copy(level, at).start()

    total[...] += in_a[level].astype(jnp.float32)

    @pl.loop(1, levels)
    def _(step):
        source = lax.rem(level + levels - step, levels)
        down_copy(source, level).wait_recv()
        total[...] += in_b[source].astype(jnp.float32)

    rounded = total[...].T.astype(jnp.bfloat16)
    sk_ref[...] = rounded
    skf[...] = rounded.astype(jnp.float32)
    blocks_piece = q_cols // ROWBLK
    nq = q_hbm.shape[0]

    def line_of(piece, block):
        line = skf[pl.ds(piece * blocks_piece + block, 1), :]
        return jnp.broadcast_to(line, (16, ROWBLK))[None]

    def piece_scores(piece, accs):
        query_copy(piece).wait()

        def body(index, accs):
            accs = list(accs)
            for extra in range(8):
                block = (index * 8 + extra) * 2
                lines = [line_of(piece, block + at) for at in range(2)]
                for top in range(0, nq, 64):
                    both = None
                    for at in range(2):
                        lanes = pl.ds(pl.multiple_of((block + at) * ROWBLK, ROWBLK), ROWBLK)
                        rows = q_box[piece, top : top + 64, lanes].reshape(64 // 16, 16, ROWBLK)
                        term = rows.astype(jnp.float32) * lines[at]
                        both = term if both is None else both + term
                    accs[top // 64] += both.reshape(64, ROWBLK).astype(jnp.float32)
            return tuple(accs)

        return lax.fori_loop(0, blocks_piece // (2 * 8), body, accs)

    zeros = tuple(jnp.zeros((64, ROWBLK), jnp.float32) for _ in range(nq // 64))
    accs = lax.fori_loop(0, q_pieces, piece_scores, zeros)
    columns = jnp.concatenate(accs, axis=0).T
    part[...] = jnp.sum(columns, axis=0, keepdims=True)

    @pl.loop(1, n)
    def _(step):
        score_copy(me, lax.rem(me + step, n)).start()

    part_in[me] = part[...]

    @pl.loop(1, n)
    def _(step):
        score_copy(lax.rem(me + step, n), me).wait_recv()

    summed = part_in[0]
    for block in range(1, n):
        summed = summed + part_in[block]
    count = score_ref.shape[1]
    spot = lax.broadcasted_iota(jnp.int32, (128, nq), 0) + me * count
    own = lax.broadcasted_iota(jnp.int32, (128, nq), 1) == spot
    column = jnp.sum(jnp.where(own, summed, 0.0), axis=1, keepdims=True)
    score_ref[...] = jnp.broadcast_to(column, (128, 128)).T[:1, :count]

    @pl.loop(1, n)
    def _(step):
        device = lax.rem(me + step, n)
        grad_copy(me, device).wait_send()
        score_copy(me, device).wait_send()

    @pl.loop(0, n)
    def _(step):
        relay_copy(step).wait_send()

    @pl.loop(1, chips)
    def _(step):
        kept_copy(me, lax.rem(me + 2 * step, n)).wait_send()

    @pl.loop(0, levels)
    def _(step):
        cross_copy(step).wait_send()

    @pl.loop(1, levels)
    def _(step):
        down_copy(level, lax.rem(level + step, levels)).wait_send()


def per_device(n, activations, output_grads, token_ids, row_signs, column_signs, kept_blocks, queries):
    items, tokens, width = activations.shape
    cols = output_grads.shape[2]
    kept_dev = kept_blocks.shape[0]
    nq = queries.shape[0]
    q_pieces = 8
    fits = (
        items == 1
        and n % 4 == 0
        and n & (n - 1) == 0
        and cols & (cols - 1) == 0
        and cols % ROWBLK == 0
        and tokens % 16 == 0
        and (2 * tokens) % 128 == 0
        and kept_dev % 128 == 0
        and nq % (8 * n) == 0
        and nq % 64 == 0
        and nq // n <= 128
        and kept_dev % (16 * q_pieces) == 0
        and queries.size * 2 <= 2**25
    )
    if not fits:
        return per_device_plain(
            activations, output_grads, token_ids, row_signs, column_signs, kept_blocks, queries
        )
    chips = n // 2
    bf16, f32 = jnp.bfloat16, jnp.float32
    dma = pltpu.SemaphoreType.DMA
    any_spec = pl.BlockSpec(memory_space=pl.ANY)
    vmem_spec = pl.BlockSpec(memory_space=pltpu.VMEM)
    sketches, scores = pl.pallas_call(
        functools.partial(kernel, n),
        out_shape=(
            jax.ShapeDtypeStruct((kept_dev, ROWBLK), bf16),
            jax.ShapeDtypeStruct((1, nq // n), f32),
        ),
        in_specs=[any_spec, any_spec, vmem_spec, vmem_spec, vmem_spec, vmem_spec, any_spec],
        out_specs=(vmem_spec, vmem_spec),
        scratch_shapes=[
            pltpu.VMEM((2 * tokens, width), bf16),
            pltpu.VMEM((n, 2 * tokens, cols), bf16),
            pltpu.VMEM((n, kept_dev // 128, 128), jnp.int32),
            pltpu.VMEM((n, 2 * tokens, cols), f32),
            pltpu.VMEM((n, cols, 2 * tokens), f32),
            pltpu.VMEM((n, 2 * tokens, cols), bf16),
            pltpu.VMEM((cols, n * 2 * tokens), bf16),
            pltpu.VMEM((n * 2 * tokens, kept_dev), bf16),
            pltpu.VMEM((chips // 2, ROWBLK, kept_dev), bf16),
            pltpu.VMEM((chips // 2, ROWBLK, kept_dev), bf16),
            pltpu.VMEM((chips // 2, ROWBLK, kept_dev), bf16),
            pltpu.VMEM((chips // 2, ROWBLK, kept_dev), bf16),
            pltpu.VMEM((ROWBLK, kept_dev), f32),
            pltpu.VMEM((q_pieces, nq, queries.shape[1] // q_pieces), bf16),
            pltpu.VMEM((kept_dev, ROWBLK), f32),
            pltpu.VMEM((1, nq), f32),
            pltpu.VMEM((n, 1, nq), f32),
            dma((2,)), dma((2,)), dma((q_pieces,)),
            dma((n,)), dma((n,)), dma((n,)), dma((n,)), dma((n,)), dma((n,)),
            dma((chips // 2,)), dma((chips // 2,)), dma((chips // 2,)), dma((chips // 2,)), dma((n,)), dma((n,)),
        ],
        compiler_params=pltpu.CompilerParams(
            collective_id=0, has_side_effects=True, vmem_limit_bytes=60 * 2**20
        ),
    )(
        activations[0],
        output_grads[0],
        token_ids,
        column_signs.reshape(-1, 128),
        row_signs.reshape(-1, 128),
        kept_blocks.reshape(-1, 128),
        queries,
    )
    return sketches.reshape(1, kept_dev * ROWBLK), scores.reshape(nq // n, 1)


def solution(mesh):
    placed = (
        P("grp", "wide", None),
        P("grp", None, "wide"),
        P("grp", None),
        P(),
        P(),
        P("wide"),
        P(None, "wide"),
    )
    return jax.shard_map(
        functools.partial(per_device, mesh.shape["wide"]),
        mesh=mesh,
        in_specs=placed,
        out_specs=(P("grp", "wide"), P("wide", "grp")),
        check_vma=False,
    )
```
